32 devices in a mesh: seq: 8 (over z, x), tp: 4 (over y, core).
Axes of the slice: x: 2, y: 2, z: 4, core: 2. Of those that a mesh axis runs over, the one named last changes fastest.
Arguments:
- inner_x: bfloat16 [4, 1024, 8192], P(None, 'seq', 'tp'), may hold values from -6 to 6
- inner_z: bfloat16 [4, 1024, 8192], P(None, 'seq', 'tp'), may hold values from -6 to 6
- conv_tail: bfloat16 [4, 3, 8192], P(None, None, 'tp'), may hold values from -6 to 6
- conv_weight: float32 [4, 8192], P(None, 'tp'), may hold values from -3 to 3
- conv_bias: float32 [8192], P('tp'), may hold values from -3 to 3
- xproj_dt: bfloat16 [8192, 512], P('tp'), may hold values from -0.0625 to 0.0625
- xproj_bc: bfloat16 [8192, 32], P('tp'), may hold values from -0.0625 to 0.0625
- dt_weight: bfloat16 [512, 8192], P(None, 'tp'), may hold values from -0.25 to 0.25
- dt_bias: float32 [8192], P('tp'), may hold values from -5 to -4
- decay_log: float32 [16, 8192], P(None, 'tp'), may hold values from -8 to 1.1
- skip_gain: float32 [8192], P('tp'), may hold values from 0.5 to 1.5
- out_weight: bfloat16 [8192, 8192], P('tp'), may hold values from -0.0625 to 0.0625
- residual: bfloat16 [4, 1024, 8192], P(None, 'seq', 'tp'), may hold values from -6 to 6
- init_state: float32 [4, 16, 8192], P(None, None, 'tp'), may hold values from -6 to 6
Outputs:
- hidden_out: bfloat16 [4, 1024, 8192], P(None, 'seq', 'tp')
- block_states: float32 [8, 4, 16, 8192], P('seq', None, None, 'tp')
The draws below stay inside these ranges and needn't reach their ends.
All inputs are finite; a program needn't handle non-finite values.
Results may differ from the reference program's by a relative error of at most 0.024.
Values may be sent and summed in bfloat16 or wider, within the bound.
No kernel may reach another device: no remote copies, remote signals or barrier semaphores. Data moves between devices by JAX's collectives and lax.ppermute only.
A program may use at most 128 MiB of HBM per device.

```python
import jax
import jax.numpy as jnp
from jax import lax

D = 8192
DI = 8192
R = 512
NS = 16
KCONV = 4
SEQS = 4
TOK_BLK = 128
LEN = 1024
N_SEQ = 8
N_TP = 4


def draw_decay_log(key, part):
    folded = jax.random.fold_in(key, 7)
    choose_key, level_key = jax.random.split(folded)
    share_slow = 0.5
    slow_mask = jax.random.bernoulli(choose_key, share_slow, (1, DI))
    levels = jax.random.uniform(level_key, (NS, DI), jnp.float32)
    slow_log = jnp.log(5.0 / LEN) + levels * jnp.log(10.0)
    fast_log = levels * jnp.log(3.0)
    return jnp.where(slow_mask, slow_log, fast_log).astype(jnp.float32)


def block_scale(stream_key, shape, pieces, smallest, largest):
    gain = 1.0
    for axis_at, blocks in pieces:
        steps = jax.random.uniform(jax.random.fold_in(jax.random.fold_in(stream_key, 6), axis_at), (blocks,), jnp.float32, smallest / len(pieces), largest / len(pieces))
        gain = gain * jnp.repeat(jnp.exp(steps), shape[axis_at] // blocks).reshape((-1,) + (1,) * (len(shape) - 1 - axis_at))
    return gain


def centred(key, extent, width, most, shards=(), held_as=jnp.bfloat16):
    gain = block_scale(key, extent, shards, -0.22, 0.18) if shards else 1.0
    entries = jax.random.normal(key, extent, jnp.float32) * width * gain
    return jnp.minimum(jnp.maximum(entries, -most), most).astype(held_as)


def setup_inputs(seed: int = 0) -> dict:
    arg_keys = jax.random.split(jax.random.key(seed), 15)
    return {
        "inner_x": centred(arg_keys[0], (SEQS, LEN, DI), 1.0, 6.0, ((1, 8), (2, 4))),
        "inner_z": centred(arg_keys[1], (SEQS, LEN, DI), 1.0, 6.0, ((1, 8), (2, 4))),
        "conv_tail": centred(arg_keys[2], (SEQS, KCONV - 1, DI), 1.0, 6.0, ((2, 4),)),
        "conv_weight": centred(arg_keys[3], (KCONV, DI), KCONV ** -0.5, 3.0, ((1, 4),), jnp.float32),
        "conv_bias": centred(arg_keys[4], (DI,), 0.5, 3.0, ((0, 4),), jnp.float32),
        "xproj_dt": centred(arg_keys[5], (DI, R), DI ** -0.5, 0.0625, ((0, 4),)),
        "xproj_bc": centred(arg_keys[6], (DI, 2 * NS), DI ** -0.5, 0.0625, ((0, 4),)),
        "dt_weight": centred(arg_keys[7], (R, DI), R ** -0.5, 0.25, ((1, 4),)),
        "dt_bias": jnp.clip(-5.0 + 1.0 * jax.random.uniform(arg_keys[8], (DI,), jnp.float32) ** block_scale(arg_keys[8], (DI,), ((0, 4),), -0.2, 0.2), -5.0, -4.0),
        "decay_log": draw_decay_log(jax.random.fold_in(arg_keys[14], 71), 0),
        "skip_gain": jnp.clip(0.5 + 1.0 * jax.random.uniform(arg_keys[10], (DI,), jnp.float32) ** block_scale(arg_keys[10], (DI,), ((0, 4),), -0.2, 0.2), 0.5, 1.5),
        "out_weight": centred(arg_keys[11], (DI, D), DI ** -0.5, 0.0625, ((0, 4),)),
        "residual": centred(arg_keys[12], (SEQS, LEN, D), 1.0, 6.0, ((1, 8), (2, 4))),
        "init_state": centred(arg_keys[13], (SEQS, NS, DI), 1.0, 6.0, ((2, 4),), jnp.float32),
    }


def matmul(left_op, right_op):
    return jnp.dot(left_op.astype(jnp.float32), right_op.astype(jnp.float32), preferred_element_type=jnp.float32)

def run_chain(initial, decay_rates, steps_dt, inputs_x, gates_b, reads_c):

    def advance(carried, packed):
        step_dt, value_x, gate_b, read_c = packed
        factor = jnp.exp(decay_rates[None, :, :] * step_dt[:, None, :])
        carried = factor * carried + (step_dt * value_x)[:, None, :] * gate_b[:, :, None]
        emitted = lax.optimization_barrier(jnp.sum(read_c[:, :, None] * carried, axis=1))
        return (carried, emitted)
    return lax.scan(advance, initial, (steps_dt, inputs_x, gates_b, reads_c), unroll=8)

def reference(inner_x, inner_z, conv_tail, conv_weight, conv_bias, xproj_dt, xproj_bc, dt_weight, dt_bias, decay_log, skip_gain, out_weight, residual, init_state):
    length = inner_x.shape[1]
    joined = jnp.concatenate([conv_tail, inner_x], axis=1).astype(jnp.float32)
    conv_mixed = conv_bias + conv_weight[0] * joined[:, 0:length, :]
    for offset in range(1, KCONV):
        conv_mixed = conv_mixed + conv_weight[offset] * joined[:, offset:offset + length, :]
    conv_act = jax.nn.silu(conv_mixed).astype(jnp.bfloat16)
    low_rank = matmul(conv_act, xproj_dt)
    bc_proj = matmul(conv_act, xproj_bc)
    normed = (low_rank * lax.rsqrt(lax.optimization_barrier(jnp.mean(low_rank * low_rank, axis=-1, keepdims=True)) + 1e-06)).astype(jnp.bfloat16)
    steps_dt = jax.nn.softplus(matmul(normed, dt_weight) + dt_bias)
    gates_b = bc_proj[..., :NS]
    reads_c = bc_proj[..., NS:]
    decay_rates = -jnp.exp(decay_log)
    values = conv_act.astype(jnp.float32)

    def to_blocks(array_in):
        return jnp.transpose(array_in, (1, 0, 2)).reshape(N_SEQ, TOK_BLK, array_in.shape[0], array_in.shape[2])

    def per_block(carried, packed):
        carried, emitted = run_chain(carried, decay_rates, packed[0], packed[1], packed[2], packed[3])
        return (carried, (carried, emitted))
    unused, (states, emitted) = lax.scan(per_block, init_state, (to_blocks(steps_dt), to_blocks(values), to_blocks(gates_b), to_blocks(reads_c)))
    scanned = jnp.transpose(emitted.reshape(length, SEQS, -1), (1, 0, 2)) + skip_gain * values
    gated_out = (scanned * jax.nn.silu(inner_z.astype(jnp.float32))).astype(jnp.bfloat16)
    group_width = DI // N_TP
    total_sum = jnp.zeros(residual.shape, jnp.float32)
    for group_index in range(N_TP):
        lower = group_index * group_width
        partial_sum = matmul(gated_out[..., lower:lower + group_width], out_weight[lower:lower + group_width]).astype(jnp.bfloat16)
        partial_sum = lax.optimization_barrier(partial_sum)
        total_sum = total_sum + partial_sum.astype(jnp.float32)
    hidden_out = (residual.astype(jnp.float32) + total_sum).astype(jnp.bfloat16)
    return (hidden_out, states)
```

```python
import functools

import jax
import jax.numpy as jnp
from jax import lax
from jax.experimental import pallas as pl
from jax.experimental.pallas import tpu as pltpu
from jax.sharding import PartitionSpec as P

LANES = 128
SUBLANES = 8
TILE = LANES * SUBLANES
LOG2E = 1.4426950408889634
VMEM_LIMIT = 40 * 2**20


def swapped(x, axis, bit):
    return lax.ppermute(x, axis, [(i, i ^ bit) for i in range(lax.axis_size(axis))])


def bits_of(axis):
    bit, found = 1, []
    while bit < lax.axis_size(axis):
        found.append(bit)
        bit *= 2
    return found


def to_rows(x):
    return x.reshape(*x.shape[:-1], -1, SUBLANES, LANES)


def spread(bc_ref, wide_ref, count):
    tokens = bc_ref.shape[0]
    for n in range(count):
        wide_ref[pl.ds(n * tokens, tokens), :] = jnp.broadcast_to(
            bc_ref[:, n : n + 1], (tokens, LANES)
        )


def scan_tokens(dt_ref, u_ref, wide_ref, rate_ref, first, states, tokens, y_ref, unroll):
    rates = [rate_ref[n] for n in range(states)]

    def group(i, held):
        held = list(held)
        for j in range(unroll):
            t = i * unroll + j
            base = i * (unroll * SUBLANES) + (j // SUBLANES) * SUBLANES * SUBLANES
            rows = pl.ds(base + j % SUBLANES, SUBLANES, stride=SUBLANES)
            dt = dt_ref[rows, :]
            u = u_ref[rows, :]
            y = None
            for n in range(states):
                gate = wide_ref[pl.ds(n * tokens + t, SUBLANES, stride=0), :]
                held[n] = jnp.exp2(rates[n] * dt) * held[n] + u * gate
                if y_ref is not None:
                    read = wide_ref[pl.ds((states + n) * tokens + t, SUBLANES, stride=0), :]
                    part = read * held[n]
                    y = part if y is None else y + part
            if y_ref is not None:
                y_ref[rows, :] = y
        return tuple(held)

    return lax.fori_loop(0, tokens // unroll, group, tuple(first))


def steps_kernel(
    states, normed_ref, weight_ref, bias_ref, act_ref, bc_ref, rate_ref,
    dt_ref, end_ref, elapsed_ref, u_ref, wide_ref,
):
    tokens = normed_ref.shape[0]
    spread(bc_ref, wide_ref, states)
    raw = jnp.dot(normed_ref[...], weight_ref[...], preferred_element_type=jnp.float32)
    raw = raw + bias_ref[...]
    dt = jnp.maximum(raw, 0.0) + jnp.log1p(jnp.exp(-jnp.abs(raw)))
    u = dt * act_ref[...].astype(jnp.float32)
    total = jnp.sum(dt, axis=0, keepdims=True)
    for g in range(SUBLANES):
        elapsed_ref[g : g + 1, :] = total[:, g * LANES : (g + 1) * LANES]
        for i in range(tokens // SUBLANES):
            rows = pl.ds((i * SUBLANES + g) * SUBLANES, SUBLANES)
            part = (slice(i * SUBLANES, (i + 1) * SUBLANES), slice(g * LANES, (g + 1) * LANES))
            dt_ref[rows, :] = dt[part]
            u_ref[rows, :] = u[part]
    zero = [jnp.zeros((SUBLANES, LANES), jnp.float32)] * states
    held = scan_tokens(dt_ref, u_ref, wide_ref, rate_ref, zero, states, tokens, None, 16)
    for n in range(states):
        end_ref[n] = held[n]


def steps_call(normed, weight, bias, act, bc, rates):
    seqs, tokens, rank = normed.shape
    tiles, states = rates.shape[0], rates.shape[1]
    sq = pl.Squeezed()
    rows = tokens * SUBLANES
    return pl.pallas_call(
        functools.partial(steps_kernel, states),
        out_shape=(
            jax.ShapeDtypeStruct((seqs, tiles, rows, LANES), jnp.float32),
            jax.ShapeDtypeStruct((seqs, tiles, states, SUBLANES, LANES), jnp.float32),
            jax.ShapeDtypeStruct((seqs, tiles, SUBLANES, LANES), jnp.float32),
        ),
        grid=(tiles, seqs),
        in_specs=[
            pl.BlockSpec((sq, tokens, rank), lambda c, s: (s, 0, 0)),
            pl.BlockSpec((rank, TILE), lambda c, s: (0, c)),
            pl.BlockSpec((1, TILE), lambda c, s: (0, c)),
            pl.BlockSpec((sq, tokens, TILE), lambda c, s: (s, 0, c)),
            pl.BlockSpec((sq, tokens, bc.shape[2]), lambda c, s: (s, 0, 0)),
            pl.BlockSpec((sq, states, SUBLANES, LANES), lambda c, s: (c, 0, 0, 0)),
        ],
        out_specs=(
            pl.BlockSpec((sq, sq, rows, LANES), lambda c, s: (s, c, 0, 0)),
            pl.BlockSpec((sq, sq, states, SUBLANES, LANES), lambda c, s: (s, c, 0, 0, 0)),
            pl.BlockSpec((sq, sq, SUBLANES, LANES), lambda c, s: (s, c, 0, 0)),
        ),
        scratch_shapes=[
            pltpu.VMEM((rows, LANES), jnp.float32),
            pltpu.VMEM((states * tokens, LANES), jnp.float32),
        ],
        compiler_params=pltpu.CompilerParams(vmem_limit_bytes=VMEM_LIMIT),
        cost_estimate=pl.CostEstimate(
            flops=2 * seqs * tokens * rank * tiles * TILE,
            bytes_accessed=8 * seqs * tokens * tiles * TILE,
            transcendentals=seqs * tokens * tiles * TILE * states,
        ),
    )(normed, weight, bias[None], act, bc, rates)


def scan_kernel(
    states, dt_ref, act_ref, z_ref, bc_ref, rate_ref, enter_ref, skip_ref,
    gated_ref, final_ref, u_ref, y_ref, wide_ref,
):
    tokens = act_ref.shape[0]
    spread(bc_ref, wide_ref, 2 * states)
    tiles = [(i, g) for i in range(tokens // SUBLANES) for g in range(SUBLANES)]

    def place(i, g):
        rows = pl.ds((i * SUBLANES + g) * SUBLANES, SUBLANES)
        return rows, pl.ds(i * SUBLANES, SUBLANES), pl.ds(g * LANES, LANES)

    for i, g in tiles:
        rows, at, lanes = place(i, g)
        u_ref[rows, :] = dt_ref[rows, :] * act_ref[at, lanes].astype(jnp.float32)
    first = [enter_ref[n] for n in range(states)]
    held = scan_tokens(dt_ref, u_ref, wide_ref, rate_ref, first, states, tokens, y_ref, 16)
    for n in range(states):
        for g in range(SUBLANES):
            final_ref[n : n + 1, g * LANES : (g + 1) * LANES] = held[n][g : g + 1, :]
    for i in range(tokens // 16):
        for g in range(SUBLANES):
            lanes = pl.ds(g * LANES, LANES)
            at = pl.ds(i * 16, 16)
            y = jnp.concatenate([y_ref[place(2 * i + k, g)[0], :] for k in range(2)], axis=0)
            y = y + skip_ref[0:1, lanes] * act_ref[at, lanes].astype(jnp.float32)
            z = z_ref[at, lanes].astype(jnp.float32)
            gated_ref[at, lanes] = (y * (z / (1.0 + jnp.exp(-z)))).astype(jnp.bfloat16)


def scan_call(dt, act, z, bc, rates, entering, skip):
    seqs, tiles, rows, _ = dt.shape
    tokens, states = act.shape[1], rates.shape[1]
    sq = pl.Squeezed()
    flat = pl.BlockSpec((sq, tokens, TILE), lambda c, s: (s, 0, c))
    return pl.pallas_call(
        functools.partial(scan_kernel, states),
        out_shape=(
            jax.ShapeDtypeStruct((seqs, tokens, tiles * TILE), jnp.bfloat16),
            jax.ShapeDtypeStruct((seqs, states, tiles * TILE), jnp.float32),
        ),
        grid=(tiles, seqs),
        in_specs=[
            pl.BlockSpec((sq, sq, rows, LANES), lambda c, s: (s, c, 0, 0)),
            flat,
            flat,
            pl.BlockSpec((sq, tokens, bc.shape[2]), lambda c, s: (s, 0, 0)),
            pl.BlockSpec((sq, states, SUBLANES, LANES), lambda c, s: (c, 0, 0, 0)),
            pl.BlockSpec((sq, sq, states, SUBLANES, LANES), lambda c, s: (s, c, 0, 0, 0)),
            pl.BlockSpec((1, TILE), lambda c, s: (0, c)),
        ],
        out_specs=(flat, pl.BlockSpec((sq, states, TILE), lambda c, s: (s, 0, c))),
        scratch_shapes=[
            pltpu.VMEM((rows, LANES), jnp.float32),
            pltpu.VMEM((rows, LANES), jnp.float32),
            pltpu.VMEM((2 * states * tokens, LANES), jnp.float32),
        ],
        compiler_params=pltpu.CompilerParams(vmem_limit_bytes=VMEM_LIMIT),
        cost_estimate=pl.CostEstimate(
            flops=6 * seqs * tokens * tiles * TILE * states,
            bytes_accessed=10 * seqs * tokens * tiles * TILE,
            transcendentals=seqs * tokens * tiles * TILE * states,
        ),
    )(dt, act, z, bc, rates, entering, skip[None])


def out_kernel(me_ref, x_ref, w_ref, o_ref):
    o_ref[...] = jnp.dot(x_ref[...], w_ref[...], preferred_element_type=jnp.float32).astype(
        o_ref.dtype
    )


def out_call(me, x, weight, groups, piece, pieces):
    rows, depth = x.shape
    own = weight.shape[1] // groups
    width = own // pieces
    step = min(width, 512)
    steps = width // step
    sq = pl.Squeezed()
    return pl.pallas_call(
        out_kernel,
        out_shape=jax.ShapeDtypeStruct((groups, rows, width), jnp.bfloat16),
        grid_spec=pltpu.PrefetchScalarGridSpec(
            num_scalar_prefetch=1,
            grid=(groups, steps),
            in_specs=[
                pl.BlockSpec((rows, depth), lambda j, k, me: (0, 0)),
                pl.BlockSpec(
                    (depth, step),
                    lambda j, k, me: (0, ((groups - 1 - j) ^ me[0]) * (own // step) + piece * steps + k),
                ),
            ],
            out_specs=pl.BlockSpec((sq, rows, step), lambda j, k, me: (groups - 1 - j, 0, k)),
        ),
        compiler_params=pltpu.CompilerParams(vmem_limit_bytes=VMEM_LIMIT),
        cost_estimate=pl.CostEstimate(
            flops=2 * rows * depth * width * groups,
            bytes_accessed=2 * depth * width * groups,
            transcendentals=0,
        ),
    )(me, x, weight)


def scattered(parts, axis):
    held = [parts]
    for bit in bits_of(axis):
        cut = [p.reshape(p.shape[0] // 2, 2, *p.shape[1:]) for p in held]
        keep = [p[:, 0] for p in cut]
        gone = functools.reduce(
            jnp.add, [p[:, 1].astype(jnp.float32) for p in cut]
        ).astype(jnp.bfloat16)
        held = keep + [swapped(gone, axis, bit)]
    return functools.reduce(jnp.add, [p[0].astype(jnp.float32) for p in held])


def carried(end, elapsed, rates):
    place = lax.axis_index("seq")
    decayed = lambda time, state: jnp.exp2(rates * time[:, :, None]) * state
    prior_time, prior = jnp.zeros_like(elapsed), jnp.zeros_like(end)
    time, state = elapsed, end
    bits = bits_of("seq")
    for bit in bits:
        high = time.astype(jnp.bfloat16)
        low = (time - high.astype(jnp.float32)).astype(jnp.bfloat16)
        sent = jnp.concatenate(
            [state.astype(jnp.bfloat16), high[:, :, None], low[:, :, None]], axis=2
        )
        came = swapped(sent, "seq", bit).astype(jnp.float32)
        their_state, their_time = came[:, :, :-2], came[:, :, -2] + came[:, :, -1]
        late = (place & bit) != 0
        prior = jnp.where(late, decayed(prior_time, their_state) + prior, prior)
        prior_time = jnp.where(late, prior_time + their_time, prior_time)
        if bit != bits[-1]:
            state = jnp.where(
                late,
                decayed(time, their_state) + state,
                decayed(their_time, state) + their_state,
            )
            time = time + their_time
    return prior_time, prior


def summed(part, axis):
    for bit in bits_of(axis):
        sent = part if bit == 1 else part.astype(jnp.bfloat16)
        part = part + swapped(sent, axis, bit).astype(jnp.float32)
    return part


def body(
    inner_x, inner_z, conv_tail, conv_weight, conv_bias, xproj_dt, xproj_bc, dt_weight, dt_bias,
    decay_log, skip_gain, out_weight, residual, init_state,
):
    seqs, length, channels = inner_x.shape
    kernel = conv_weight.shape[0]
    states = init_state.shape[1]
    rank = xproj_dt.shape[1]
    groups = lax.axis_size("tp")
    chunks = 2
    pieces = 2
    per = seqs // chunks
    me = lax.axis_index("tp").astype(jnp.int32)[None]

    rim = inner_x[:, length - (kernel - 1) :, :]
    blocks = lax.axis_size("seq")
    arrived = lax.ppermute(rim, "seq", [(i, i + 1) for i in range(blocks - 1)])
    earlier = jnp.where(lax.axis_index("seq") == 0, conv_tail, arrived)
    xproj = jnp.concatenate([xproj_dt, xproj_bc], axis=1)
    rates = jnp.swapaxes(to_rows(-jnp.exp(decay_log) * LOG2E), 0, 1)
    start = jnp.swapaxes(to_rows(init_state), 1, 2)

    acts, gates, times, ends, elapsed = [], [], [], [], []
    for c in range(chunks):
        mine = slice(c * per, (c + 1) * per)
        joined = jnp.concatenate([earlier[mine], inner_x[mine]], axis=1).astype(jnp.float32)
        mixed = conv_bias + conv_weight[0] * joined[:, 0:length, :]
        for offset in range(1, kernel):
            mixed = mixed + conv_weight[offset] * joined[:, offset : offset + length, :]
        act = jax.nn.silu(mixed).astype(jnp.bfloat16)
        part = jnp.dot(act, xproj, preferred_element_type=jnp.float32)
        both = summed(part, "tp")
        low, bc = both[..., :rank], both[..., rank:]
        normed = (
            low * lax.rsqrt(jnp.mean(low * low, axis=-1, keepdims=True) + 1e-06)
        ).astype(jnp.bfloat16)
        dt, end, time = steps_call(normed, dt_weight, dt_bias, act, bc, rates)
        acts.append(act)
        gates.append(bc)
        times.append(dt)
        ends.append(end)
        elapsed.append(time)
    hidden, finals = [], []
    for c in range(chunks):
        mine = slice(c * per, (c + 1) * per)
        prior_time, prior = carried(ends[c], elapsed[c], rates)
        entering = jnp.exp2(rates * prior_time[:, :, None]) * start[mine] + prior
        gated, final = scan_call(
            times[c], acts[c], inner_z[mine], gates[c], rates, entering, skip_gain
        )
        finals.append(final)
        flat = gated.reshape(-1, channels)
        outs = []
        for p in range(pieces):
            own = scattered(out_call(me, flat, out_weight, groups, p, pieces), "tp")
            width = own.shape[-1]
            base = residual[mine, :, p * width : (p + 1) * width].astype(jnp.float32)
            outs.append((base + own.reshape(base.shape)).astype(jnp.bfloat16))
        hidden.append(jnp.concatenate(outs, axis=-1))
    return jnp.concatenate(hidden, axis=0), jnp.concatenate(finals, axis=0)[None]


def solution(mesh):
    return jax.shard_map(
        body,
        mesh=mesh,
        in_specs=(
            P(None, "seq", "tp"),
            P(None, "seq", "tp"),
            P(None, None, "tp"),
            P(None, "tp"),
            P("tp"),
            P("tp", None),
            P("tp", None),
            P(None, "tp"),
            P("tp"),
            P(None, "tp"),
            P("tp"),
            P("tp", None),
            P(None, "seq", "tp"),
            P(None, None, "tp"),
        ),
        out_specs=(P(None, "seq", "tp"), P("seq", None, None, "tp")),
        check_vma=False,
    )
```
